128 devices in a mesh: clients: 16 (over x, y_hi, core), shard: 8 (over z, y_lo).
Axes of the slice: x: 4, y: 4 (y_hi: 2, y_lo: 2; y = y_hi * 2 + y_lo), z: 4, core: 2. Of those that a mesh axis runs over, the one named last changes fastest.
Arguments:
- client_deltas: bfloat16 [256, 128, 3584], P(('clients', 'shard')), may hold values from -24 to 24
- variate_deltas: bfloat16 [256, 128, 3584], P(('clients', 'shard')), may hold values from -6 to 6
- params: float32 [128, 3584], P(('clients', 'shard')), may hold values from -1.5 to 1.5
- variate: float32 [128, 3584], P(('clients', 'shard')), may hold values from -1.5 to 1.5
- taking_part: int32 [256], P(('clients', 'shard')), may hold values from 0 to 1, as said below
- counts: int32 [256], P(('clients', 'shard')), may hold values from 32 to 287
Outputs:
- new_params: float32 [128, 3584], P(('clients', 'shard'))
- new_variate: float32 [128, 3584], P(('clients', 'shard'))
- client_params: bfloat16 [128, 3584], replicated
- client_variate: bfloat16 [128, 3584], replicated
The draws below stay inside these ranges and needn't reach their ends.
Inputs may be any that keep to these rules, and one draw needn't show every extreme that they name: `taking_part`: at least one client takes part.
All inputs are finite; a program needn't handle non-finite values.
Results may differ from the reference program's by a relative error of at most 0.001.
Values may be sent and summed in bfloat16 or wider, within the bound.
No kernel may reach another device: no remote copies, remote signals or barrier semaphores. Data moves between devices by JAX's collectives and lax.ppermute only.
A program may use at most 64 MiB of HBM per device.

```python
import jax
import jax.numpy as jnp

D = 3584
CLIENTS = 256
ROWS = 128


def draw_taking_part(key, part):
    random_bits = jax.random.randint(jax.random.fold_in(key, 11), (CLIENTS,), 0, 2)
    picked = jax.random.randint(jax.random.fold_in(key, 12), (), 0, CLIENTS)
    return jnp.where(jnp.arange(CLIENTS) == picked, 1, random_bits).astype(jnp.int32)


def draw_counts(key, part):
    base_count = jax.random.randint(jax.random.fold_in(key, 21), (CLIENTS,), 32, 97)
    return (base_count + 192 * jnp.arange(CLIENTS) // CLIENTS).astype(jnp.int32)


def spiked(values, key, source, target, blocks, factor):
    def block_of(axis_at):
        return (jnp.arange(values.shape[axis_at]) // (values.shape[axis_at] // blocks)).reshape((-1,) + (1,) * (values.ndim - 1 - axis_at))

    one_side = jax.random.permutation(key, blocks)[block_of(target)]
    other_side = (block_of(target) + blocks // 2) % blocks
    return jnp.where((block_of(source) == one_side) | (block_of(source) == other_side), factor * values, values)


def level_of(key, shape, split, low, top_value):
    def one(axis_at, shards_of):
        heights = jax.random.uniform(jax.random.fold_in(jax.random.fold_in(key, 6), axis_at), (shards_of,), jnp.float32, low / len(split), top_value / len(split))
        return jnp.repeat(jnp.exp(heights), shape[axis_at] // shards_of).reshape((-1,) + (1,) * (len(shape) - axis_at - 1))

    loudness = one(*split[0])
    for cut in split[1:]:
        loudness = loudness * one(*cut)
    return loudness


def centred(stream_key, shape, scale, reach, shards=(), held_as=jnp.bfloat16):
    entries = scale * jax.random.normal(stream_key, shape, jnp.float32)
    if shards:
        entries = entries * level_of(stream_key, shape, shards, -0.22, 0.18)
    return jnp.clip(entries, -reach, reach).astype(held_as)


def bell_draw_with(key, shape, scale, limit, shards, heavy, held_as=jnp.bfloat16):
    array = scale * jax.random.normal(key, shape, jnp.float32)
    if shards:
        array = array * level_of(key, shape, shards, -0.22, 0.18)
    return jnp.clip(spiked(array, jax.random.fold_in(key, 3), *heavy), -limit, limit).astype(held_as)


def setup_inputs(seed: int = 0) -> dict:
    keys = jax.random.split(jax.random.key(seed), 7)
    return {
        "client_deltas": bell_draw_with(keys[0], (CLIENTS, ROWS, D), 1.0, 24.0, ((0, 128),), (0, 1, 128, 5.5)),
        "variate_deltas": centred(keys[1], (CLIENTS, ROWS, D), 1.0, 6.0, ((0, 128),)),
        "params": centred(keys[2], (ROWS, D), 0.1, 1.5, ((0, 128),), jnp.float32),
        "variate": centred(keys[3], (ROWS, D), 0.1, 1.5, ((0, 128),), jnp.float32),
        "taking_part": draw_taking_part(jax.random.fold_in(keys[6], 71), 0),
        "counts": draw_counts(jax.random.fold_in(keys[6], 71), 0),
    }


def reference(client_deltas, variate_deltas, params, variate, taking_part, counts):
    weight = taking_part * counts
    upper_part = (weight // 16) * 16
    lower_part = weight - upper_part
    weight_table = jnp.stack([upper_part, lower_part]).astype(jnp.bfloat16)
    weight_total = jnp.sum(weight).astype(jnp.float32)
    moved_sum = jnp.dot(weight_table, client_deltas.reshape(CLIENTS, -1), preferred_element_type=jnp.float32)
    summed = (moved_sum[0] + moved_sum[1]).reshape(ROWS, D)
    chosen = taking_part.astype(jnp.bfloat16)[None, :]
    shifted = jnp.dot(chosen, variate_deltas.reshape(CLIENTS, -1), preferred_element_type=jnp.float32).reshape(ROWS, D)
    new_params = params + summed / weight_total
    new_variate = variate + shifted / jnp.float32(CLIENTS)
    return new_params, new_variate, new_params.astype(jnp.bfloat16), new_variate.astype(jnp.bfloat16)
```

```python
import functools

import jax
import jax.numpy as jnp
from jax import lax
from jax.experimental import pallas as pl
from jax.experimental.pallas import tpu as pltpu
from jax.sharding import Mesh
from jax.sharding import PartitionSpec as P

FINE = (("x", 4), ("yh", 2), ("core", 2), ("z", 4), ("yl", 2))
ALL = ("x", "yh", "core", "z", "yl")
CHIPS = ("x", "yh", "z", "yl")
N_CHIPS = 64
LANES = 128


def core_swap(x):
    return lax.ppermute(x, "core", [(0, 1), (1, 0)])


def weigh_kernel(scalars, deltas, changes, keep, send):
    core = scalars[0]
    w0 = scalars[1].astype(jnp.float32)
    w1 = scalars[2].astype(jnp.float32)
    t0 = scalars[3].astype(jnp.float32)
    t1 = scalars[4].astype(jnp.float32)
    pieces = deltas.shape[2] // LANES
    per_block = keep.shape[0] // 8

    def fill(out, source, a0, a1, tail):
        for half in range(2):
            rows = pl.ds(half * 8, 8)
            for j in range(pieces):
                lanes = pl.ds(j * LANES, LANES)
                value = source[0, rows, lanes].astype(jnp.float32) * a0
                value = value + source[1, rows, lanes].astype(jnp.float32) * a1
                out[pl.ds(half * pieces + j, 8, stride=per_block), :] = value
        for block in range(8):
            out[pl.ds(block * per_block + 2 * pieces, 8), :] = jnp.full((8, LANES), tail)

    @pl.when(core == 0)
    def _():
        fill(keep, deltas, w0, w1, w0 + w1)
        fill(send, changes, t0, t1, 0.0)

    @pl.when(core == 1)
    def _():
        fill(send, deltas, w0, w1, w0 + w1)
        fill(keep, changes, t0, t1, 0.0)


def weigh(scalars, deltas, changes):
    rows, columns = deltas.shape[1:]
    per_block = 2 * columns // LANES + 8
    in_spec = pl.BlockSpec((2, 16, columns), lambda i, s: (0, i, 0))
    out_spec = pl.BlockSpec((8 * per_block, LANES), lambda i, s: (i, 0))
    out = jax.ShapeDtypeStruct((rows // 16 * 8 * per_block, LANES), jnp.float32)
    return pl.pallas_call(
        weigh_kernel,
        grid_spec=pltpu.PrefetchScalarGridSpec(
            num_scalar_prefetch=1,
            grid=(rows // 16,),
            in_specs=[in_spec, in_spec],
            out_specs=[out_spec, out_spec],
        ),
        out_shape=[out, out],
        name="weigh",
    )(scalars, deltas, changes)


def update_kernel(client_count, core_ref, blocks, base, new, rounded):
    total = blocks[0]
    for k in range(1, blocks.shape[0]):
        total = total + blocks[k]
    used = base.shape[0]
    weight = jnp.broadcast_to(total[used : used + 1], (1, LANES))
    divisor = jnp.where(core_ref[0] == 0, weight, jnp.float32(client_count))
    fresh = base[...] + total[:used] / divisor
    new[...] = fresh
    rounded[...] = fresh.astype(jnp.bfloat16)


def update(core, blocks, base, client_count):
    vmem = pl.BlockSpec(memory_space=pltpu.VMEM)
    return pl.pallas_call(
        functools.partial(update_kernel, client_count),
        in_specs=[pl.BlockSpec(memory_space=pltpu.SMEM), vmem, vmem],
        out_specs=[vmem, vmem],
        out_shape=[
            jax.ShapeDtypeStruct(base.shape, jnp.float32),
            jax.ShapeDtypeStruct(base.shape, jnp.bfloat16),
        ],
        name="update",
    )(core, blocks, base)


def to_rows(gathered):
    parts = gathered.reshape(8, 8, 2, -1)
    return jnp.transpose(parts, (0, 2, 1, 3)).reshape(128, -1)


def body(client_deltas, variate_deltas, params, variate, taking_part, counts):
    core = lax.axis_index("core").astype(jnp.int32)
    first = core == 0
    weight = taking_part * counts
    client_count = 2 * 128
    pieces = params.shape[1] // LANES

    scalars = jnp.concatenate([core[None], weight, taking_part])
    keep, send = weigh(scalars, client_deltas, variate_deltas)

    own_base = jnp.where(first, params, variate)
    other_base = core_swap(jnp.where(first, variate, params))
    base = jnp.concatenate(
        [jnp.where(first, own_base, other_base), jnp.where(first, other_base, own_base)]
    ).reshape(2 * pieces, LANES)

    both = (keep + core_swap(send)).reshape(N_CHIPS, -1, LANES)
    blocks = lax.all_to_all(both, CHIPS, 0, 0, tiled=True)
    new, rounded = update(core[None], blocks, base, client_count)

    new = new.reshape(2, -1)
    other_new = core_swap(jnp.where(first, new[1:], new[:1]))
    own_new = jnp.where(first, new[:1], new[1:])
    new_params = jnp.where(first, own_new, other_new)
    new_variate = jnp.where(first, other_new, own_new)

    spread = jnp.broadcast_to(rounded[None], (N_CHIPS, *rounded.shape))
    gathered = lax.all_to_all(spread, CHIPS, 0, 0, tiled=True)
    swapped = core_swap(gathered)
    own_rows = to_rows(gathered)
    other_rows = to_rows(swapped)
    client_params = jnp.where(first, own_rows, other_rows)
    client_variate = jnp.where(first, other_rows, own_rows)
    return (new_params, new_variate, client_params, client_variate)


def solution(mesh):
    fine = Mesh(mesh.devices.reshape([n for _, n in FINE]), [a for a, _ in FINE])
    in_specs = (
        P(ALL, None, None),
        P(ALL, None, None),
        P(ALL, None),
        P(ALL, None),
        P(ALL),
        P(ALL),
    )
    out_specs = (P(ALL, None), P(ALL, None), P(), P())
    return jax.shard_map(body, mesh=fine, in_specs=in_specs, out_specs=out_specs, check_vma=False)
```

```python
import functools

import jax
import jax.numpy as jnp
from jax import lax
from jax.experimental import pallas as pl
from jax.experimental.pallas import tpu as pltpu
from jax.sharding import Mesh
from jax.sharding import PartitionSpec as P

AXIS = "d"
LANES = 128
CHIPS = 64


def device(i, core, s):
    return (i * 2 + core) * 8 + s


def place(d):
    return d // 16, d // 8 % 2, d % 8


def swap_pairs():
    pairs = []
    for d in range(128):
        i, core, s = place(d)
        pairs.append((d, device(i, 1 - core, s)))
    return pairs


def ring_pairs(step):
    pairs = []
    for d in range(128):
        i, core, s = place(d)
        if core == 0:
            pairs.append((d, device((i + 2 * step) % 8, core, s)))
        else:
            pairs.append((d, device(i, core, (s + 2 * step) % 8)))
    return pairs


def plane_groups():
    groups = [[device(2 * x + h, 0, s) for h in range(2) for s in range(8)] for x in range(4)]
    groups += [[device(i, 1, 2 * z + low) for low in range(2) for i in range(8)] for z in range(4)]
    return groups


def chip_groups():
    return [[device(i, core, s) for i in range(8) for s in range(8)] for core in range(2)]


def core_swap(x):
    return lax.ppermute(x, AXIS, swap_pairs())


def vmem(x):
    return pltpu.with_memory_space_constraint(x, pltpu.VMEM)


def hbm(x):
    return pltpu.with_memory_space_constraint(x, pltpu.HBM)


VMEM_SPEC = pl.BlockSpec(memory_space=pltpu.VMEM)
SMEM_SPEC = pl.BlockSpec(memory_space=pltpu.SMEM)
HBM_SPEC = pl.BlockSpec(memory_space=pltpu.HBM)
SCOPED = pltpu.CompilerParams(vmem_limit_bytes=8 * 2**20)


def my_core():
    return lax.axis_index(AXIS) // 8 % 2


def my_ring():
    d = lax.axis_index(AXIS)
    return jnp.where(d // 8 % 2 == 0, d // 32, d % 8 // 2)


def weigh_kernel(other, taking, counts, deltas, changes, out, held, arrived):
    core = my_core()
    owner = 1 - core if other else core
    chunks, pieces = held.shape[0], held.shape[3] // LANES
    block = 2 * pieces
    group = 8 * block + 8

    def fetch(source):
        for i in range(chunks):
            pltpu.make_async_copy(
                source.at[:, pl.ds(16 * i, 16), :], held.at[i], arrived.at[i]
            ).start()

    def fill(a0, a1, tail, by_chunk, by_row):
        for g in range(8):
            out[pl.ds(g * group + 8 * block, 8), :] = jnp.full((8, LANES), tail)

        def one(i, carry):
            pltpu.make_async_copy(
                deltas.at[:, pl.ds(0, 16), :], held.at[i], arrived.at[i]
            ).wait()
            for half in range(2):
                rows = pl.ds(half * 8, 8)
                for j in range(pieces):
                    lanes = pl.ds(j * LANES, LANES)
                    value = held[i, 0, rows, lanes].astype(jnp.float32) * a0
                    value = value + held[i, 1, rows, lanes].astype(jnp.float32) * a1
                    start = i * by_chunk + half * pieces + j
                    out[pl.ds(start, 8, stride=by_row), :] = value
            return carry

        lax.fori_loop(0, chunks, one, 0)

    t0, t1 = taking[0], taking[1]
    w0, w1 = t0 * counts[0], t1 * counts[1]

    @pl.when(owner == 0)
    def _():
        fetch(deltas)
        total = (w0 + w1).astype(jnp.float32)
        fill(w0.astype(jnp.float32), w1.astype(jnp.float32), total, group, block)

    @pl.when(owner == 1)
    def _():
        fetch(changes)
        fill(t0.astype(jnp.float32), t1.astype(jnp.float32), jnp.float32(0), block, group)


def weigh(other, taking, counts, deltas, changes):
    rows, columns = deltas.shape[1:]
    out_rows = 8 * (8 * 2 * columns // LANES + 8)
    return pl.pallas_call(
        functools.partial(weigh_kernel, other),
        in_specs=[SMEM_SPEC, SMEM_SPEC, HBM_SPEC, HBM_SPEC],
        out_specs=VMEM_SPEC,
        out_shape=pltpu.VMEM((out_rows, LANES), jnp.float32),
        scratch_shapes=[
            pltpu.VMEM((rows // 16, 2, 16, columns), deltas.dtype),
            pltpu.SemaphoreType.DMA((rows // 16,)),
        ],
        compiler_params=SCOPED,
        name="weigh_other" if other else "weigh_own",
    )(taking, counts, hbm(deltas), hbm(changes))


def join_kernel(keep, came, *outs):
    rows = outs[0].shape[0]
    mine = my_ring()
    for step, out in zip((2, 1, 3, 0), outs):
        at = pl.ds(pl.multiple_of((mine + step) % 4 * rows, 8), rows)
        out[...] = keep[at, :] + came[at, :]


def join(keep, came):
    out = pltpu.VMEM((keep.shape[0] // 4, LANES), jnp.float32)
    return pl.pallas_call(
        join_kernel,
        in_specs=[VMEM_SPEC, VMEM_SPEC],
        out_specs=[VMEM_SPEC] * 4,
        out_shape=[out] * 4,
        compiler_params=SCOPED,
        name="join",
    )(vmem(keep), vmem(came))


def fold_kernel(first, second, third, own, out):
    group = own.shape[0] // 2
    block = (group - 8) // 8

    def total(at, size):
        here = pl.ds(at, size)
        return own[here, :] + first[here, :] + second[here, :] + third[here, :]

    for g in range(2):
        tail = total(g * group + 8 * block, 8)
        for b in range(8):
            out[g * 8 + b, pl.ds(0, block), :] = total(g * group + b * block, block)
            out[g * 8 + b, pl.ds(block, 8), :] = tail


def fold(parts):
    group = parts[0].shape[0] // 2
    block = (group - 8) // 8
    return pl.pallas_call(
        fold_kernel,
        in_specs=[VMEM_SPEC] * 4,
        out_specs=VMEM_SPEC,
        out_shape=pltpu.VMEM((16, block + 8, LANES), jnp.float32),
        compiler_params=SCOPED,
        name="fold",
    )(*[vmem(p) for p in parts])


def update_kernel(client_count, blocks, params, variate, base, own, other, spread, total, fresh):
    core = my_core()
    count, used = blocks.shape[0], blocks.shape[1] - 8
    pieces = used // 2
    sums = blocks[0]
    for k in range(1, count):
        sums = sums + blocks[k]
    divisor = jnp.where(core == 0, sums[used : used + 1], jnp.float32(client_count))
    total[...] = sums[:used] / divisor
    for j in range(pieces):
        lanes = pl.ds(j * LANES, LANES)
        mine = jnp.where(core == 0, params[:, lanes], variate[:, lanes])
        mine = mine + total[pl.ds(core * pieces + j, 1), :]
        theirs = base[:, lanes] + total[pl.ds((1 - core) * pieces + j, 1), :]
        own[:, lanes] = mine
        other[:, lanes] = theirs
        fresh[pl.ds(core * pieces + j, 1), :] = mine
        fresh[pl.ds((1 - core) * pieces + j, 1), :] = theirs
    rounded = fresh[...].astype(jnp.bfloat16)
    for k in range(CHIPS):
        spread[k] = rounded


def update(blocks, params, variate, base, client_count):
    used = blocks.shape[1] - 8
    row = pltpu.VMEM(params.shape, jnp.float32)
    return pl.pallas_call(
        functools.partial(update_kernel, client_count),
        in_specs=[VMEM_SPEC] * 4,
        out_specs=[VMEM_SPEC] * 3,
        out_shape=[row, row, pltpu.VMEM((CHIPS, used, LANES), jnp.bfloat16)],
        scratch_shapes=[pltpu.VMEM((used, LANES), jnp.float32)] * 2,
        compiler_params=SCOPED,
        name="update",
    )(vmem(blocks), params, variate, vmem(base))


def to_rows(gathered):
    parts = gathered.reshape(8, 8, 2, -1)
    return jnp.transpose(parts, (0, 2, 1, 3)).reshape(128, -1)


def body(client_deltas, variate_deltas, params, variate, taking_part, counts):
    first = my_core() == 0
    client_count = 2 * 128

    send = weigh(True, taking_part, counts, client_deltas, variate_deltas)
    came = core_swap(send)
    keep = weigh(False, taking_part, counts, client_deltas, variate_deltas)
    base = core_swap(jnp.where(first, variate, params))

    *quarters, own_quarter = join(keep, came)
    arrived = [lax.ppermute(vmem(q), AXIS, ring_pairs(k)) for q, k in zip(quarters, (2, 1, 3))]
    plane = fold([*arrived, own_quarter])
    blocks = lax.all_to_all(vmem(plane), AXIS, 0, 0, axis_index_groups=plane_groups(), tiled=True)
    own_new, sent_new, spread = update(blocks, params, variate, base, client_count)

    other_new = core_swap(sent_new)
    new_params = jnp.where(first, own_new, other_new)
    new_variate = jnp.where(first, other_new, own_new)

    gathered = lax.all_to_all(spread, AXIS, 0, 0, axis_index_groups=chip_groups(), tiled=True)
    own_rows = to_rows(gathered)
    other_rows = to_rows(core_swap(gathered))
    client_params = jnp.where(first, own_rows, other_rows)
    client_variate = jnp.where(first, other_rows, own_rows)
    return (new_params, new_variate, client_params, client_variate)


def solution(mesh):
    flat = Mesh(mesh.devices.reshape(-1), (AXIS,))
    split = P(AXIS)
    in_specs = (split, split, split, split, split, split)
    out_specs = (split, split, P(), P())
    return jax.shard_map(body, mesh=flat, in_specs=in_specs, out_specs=out_specs, check_vma=False)
```

```python
import functools

import jax
import jax.numpy as jnp
from jax import lax
from jax.experimental import pallas as pl
from jax.experimental.pallas import tpu as pltpu
from jax.sharding import Mesh
from jax.sharding import PartitionSpec as P

AXIS = "d"
LANES = 128
CHIPS = 64


def device(i, core, s):
    return (i * 2 + core) * 8 + s


def place(d):
    return d // 16, d // 8 % 2, d % 8


def swap_pairs():
    pairs = []
    for d in range(128):
        i, core, s = place(d)
        pairs.append((d, device(i, 1 - core, s)))
    return pairs


def ring_pairs(step):
    pairs = []
    for d in range(128):
        i, core, s = place(d)
        if core == 0:
            pairs.append((d, device((i + 2 * step) % 8, core, s)))
        else:
            pairs.append((d, device(i, core, (s + 2 * step) % 8)))
    return pairs


def plane_groups():
    groups = [[device(2 * x + h, 0, s) for h in range(2) for s in range(8)] for x in range(4)]
    groups += [[device(i, 1, 2 * z + low) for low in range(2) for i in range(8)] for z in range(4)]
    return groups


def chip_groups():
    return [[device(i, core, s) for i in range(8) for s in range(8)] for core in range(2)]


def core_swap(x):
    return lax.ppermute(x, AXIS, swap_pairs())


def vmem(x):
    return pltpu.with_memory_space_constraint(x, pltpu.VMEM)


def hbm(x):
    return pltpu.with_memory_space_constraint(x, pltpu.HBM)


VMEM_SPEC = pl.BlockSpec(memory_space=pltpu.VMEM)
HBM_SPEC = pl.BlockSpec(memory_space=pltpu.HBM)
SCOPED = pltpu.CompilerParams(vmem_limit_bytes=8 * 2**20)


def my_core():
    return lax.axis_index(AXIS) // 8 % 2


def my_ring():
    d = lax.axis_index(AXIS)
    return jnp.where(d // 8 % 2 == 0, d // 32, d % 8 // 2)


def weigh_kernel(
    other, taking_hbm, counts_hbm, deltas, changes, out, held, taking, counts, arrived, small
):
    core = my_core()
    owner = 1 - core if other else core
    chunks, pieces = held.shape[0], held.shape[3] // LANES
    block = 2 * pieces
    group = 8 * block + 8

    def fetch(source):
        for i in range(chunks):
            pltpu.make_async_copy(
                source.at[:, pl.ds(16 * i, 16), :], held.at[i], arrived.at[i]
            ).start()

    def fill(a0, a1, tail, by_chunk, by_row):
        for g in range(8):
            out[pl.ds(g * group + 8 * block, 8), :] = jnp.full((8, LANES), tail)

        def one(i, carry):
            pltpu.make_async_copy(
                deltas.at[:, pl.ds(0, 16), :], held.at[i], arrived.at[i]
            ).wait()
            for half in range(2):
                rows = pl.ds(half * 8, 8)
                for j in range(pieces):
                    lanes = pl.ds(j * LANES, LANES)
                    value = held[i, 0, rows, lanes].astype(jnp.float32) * a0
                    value = value + held[i, 1, rows, lanes].astype(jnp.float32) * a1
                    start = i * by_chunk + half * pieces + j
                    out[pl.ds(start, 8, stride=by_row), :] = value
            return carry

        lax.fori_loop(0, chunks, one, 0)

    scalars = [
        pltpu.make_async_copy(taking_hbm, taking, small.at[0]),
        pltpu.make_async_copy(counts_hbm, counts, small.at[1]),
    ]
    for copy in scalars:
        copy.start()

    @pl.when(owner == 0)
    def _():
        fetch(deltas)

    @pl.when(owner == 1)
    def _():
        fetch(changes)

    for copy in scalars:
        copy.wait()
    t0, t1 = taking[0], taking[1]
    w0, w1 = t0 * counts[0], t1 * counts[1]

    @pl.when(owner == 0)
    def _():
        total = (w0 + w1).astype(jnp.float32)
        fill(w0.astype(jnp.float32), w1.astype(jnp.float32), total, group, block)

    @pl.when(owner == 1)
    def _():
        fill(t0.astype(jnp.float32), t1.astype(jnp.float32), jnp.float32(0), block, group)


def weigh(other, taking, counts, deltas, changes):
    rows, columns = deltas.shape[1:]
    out_rows = 8 * (8 * 2 * columns // LANES + 8)
    return pl.pallas_call(
        functools.partial(weigh_kernel, other),
        in_specs=[HBM_SPEC] * 4,
        out_specs=VMEM_SPEC,
        out_shape=pltpu.VMEM((out_rows, LANES), jnp.float32),
        scratch_shapes=[
            pltpu.VMEM((rows // 16, 2, 16, columns), deltas.dtype),
            pltpu.SMEM(taking.shape, jnp.int32),
            pltpu.SMEM(counts.shape, jnp.int32),
            pltpu.SemaphoreType.DMA((rows // 16,)),
            pltpu.SemaphoreType.DMA((2,)),
        ],
        compiler_params=SCOPED,
        name="weigh_other" if other else "weigh_own",
    )(hbm(taking), hbm(counts), hbm(deltas), hbm(changes))


def join_kernel(keep, came, *outs):
    rows = outs[0].shape[0]
    mine = my_ring()
    for step, out in zip((1, 3, 2, 0), outs):
        at = pl.ds(pl.multiple_of((mine + step) % 4 * rows, 8), rows)
        out[...] = keep[at, :] + came[at, :]


def join(keep, came):
    out = pltpu.VMEM((keep.shape[0] // 4, LANES), jnp.float32)
    return pl.pallas_call(
        join_kernel,
        in_specs=[VMEM_SPEC, VMEM_SPEC],
        out_specs=[VMEM_SPEC] * 4,
        out_shape=[out] * 4,
        compiler_params=SCOPED,
        name="join",
    )(vmem(keep), vmem(came))


def fold_kernel(first, second, third, own, out):
    group = own.shape[0] // 2
    block = (group - 8) // 8

    def total(at, size):
        here = pl.ds(at, size)
        return own[here, :] + first[here, :] + second[here, :] + third[here, :]

    for g in range(2):
        tail = total(g * group + 8 * block, 8)
        for b in range(8):
            out[g * 8 + b, pl.ds(0, block), :] = total(g * group + b * block, block)
            out[g * 8 + b, pl.ds(block, 8), :] = tail


def fold(parts):
    group = parts[0].shape[0] // 2
    block = (group - 8) // 8
    return pl.pallas_call(
        fold_kernel,
        in_specs=[VMEM_SPEC] * 4,
        out_specs=VMEM_SPEC,
        out_shape=pltpu.VMEM((16, block + 8, LANES), jnp.float32),
        compiler_params=SCOPED,
        name="fold",
    )(*[vmem(p) for p in parts])


def update_kernel(client_count, blocks, params, variate, base, own, other, spread, total, fresh):
    core = my_core()
    count, used = blocks.shape[0], blocks.shape[1] - 8
    pieces = used // 2
    sums = blocks[0]
    for k in range(1, count):
        sums = sums + blocks[k]
    divisor = jnp.where(core == 0, sums[used : used + 1], jnp.float32(client_count))
    total[...] = sums[:used] / divisor
    for j in range(pieces):
        lanes = pl.ds(j * LANES, LANES)
        mine = jnp.where(core == 0, params[:, lanes], variate[:, lanes])
        mine = mine + total[pl.ds(core * pieces + j, 1), :]
        theirs = base[:, lanes] + total[pl.ds((1 - core) * pieces + j, 1), :]
        own[:, lanes] = mine
        other[:, lanes] = theirs
        fresh[pl.ds(core * pieces + j, 1), :] = mine
        fresh[pl.ds((1 - core) * pieces + j, 1), :] = theirs
    rounded = fresh[...].astype(jnp.bfloat16)
    for k in range(CHIPS):
        spread[k] = rounded


def update(blocks, params, variate, base, client_count):
    used = blocks.shape[1] - 8
    row = pltpu.VMEM(params.shape, jnp.float32)
    return pl.pallas_call(
        functools.partial(update_kernel, client_count),
        in_specs=[VMEM_SPEC] * 4,
        out_specs=[VMEM_SPEC] * 3,
        out_shape=[row, row, pltpu.VMEM((CHIPS, used, LANES), jnp.bfloat16)],
        scratch_shapes=[pltpu.VMEM((used, LANES), jnp.float32)] * 2,
        compiler_params=SCOPED,
        name="update",
    )(vmem(blocks), params, variate, vmem(base))


def lay_out(source, wide, put, done=lambda i: None):
    chips, block = source.shape[:2]
    pieces = block // 2
    for k in range(chips):
        wide[pl.ds(k * block, block), :] = source[k].astype(jnp.float32)

    def one(i, carry):
        for j in range(pieces):
            rows = [wide[pl.ds(i * 8 * block + c * pieces + j, 8, stride=block), :] for c in (0, 1)]
            put(i, j, jnp.concatenate(rows).astype(jnp.bfloat16))
        done(i)
        return carry

    lax.fori_loop(0, 8, one, 0)


def lay_kernel(source, out, wide):
    def put(i, j, value):
        at = pl.ds(pl.multiple_of(i * 16, 16), 16)
        out[at, pl.ds(j * LANES, LANES)] = value

    lay_out(source, wide, put)


def lay(gathered):
    chips, block = gathered.shape[:2]
    return pl.pallas_call(
        lay_kernel,
        in_specs=[VMEM_SPEC],
        out_specs=VMEM_SPEC,
        out_shape=pltpu.VMEM((2 * chips, block // 2 * LANES), jnp.bfloat16),
        scratch_shapes=[pltpu.VMEM((chips * block, LANES), jnp.float32)],
        compiler_params=SCOPED,
        name="lay",
    )(vmem(gathered))


def finish_kernel(own_rows, swapped, own_new, other_new, *refs):
    outs, wide, laid, sems = refs[:4], refs[4], refs[5], refs[6]
    core = my_core()

    def place_all(mine, theirs, mine_rows, their_rows):
        copies = [
            pltpu.make_async_copy(own_new, mine, sems.at[0]),
            pltpu.make_async_copy(other_new, theirs, sems.at[1]),
            pltpu.make_async_copy(own_rows, mine_rows, sems.at[2]),
        ]
        for copy in copies:
            copy.start()

        def put(i, j, value):
            at = pl.ds(pl.multiple_of(i * 16, 16), 16)
            laid[at, pl.ds(j * LANES, LANES)] = value

        def write(i):
            at = pl.ds(pl.multiple_of(i * 16, 16), 16)
            return pltpu.make_async_copy(laid.at[at, :], their_rows.at[at, :], sems.at[3 + i])

        lay_out(swapped, wide, put, lambda i: write(i).start())
        for copy in copies:
            copy.wait()
        for i in range(8):
            write(i).wait()

    @pl.when(core == 0)
    def _():
        place_all(outs[0], outs[1], outs[2], outs[3])

    @pl.when(core == 1)
    def _():
        place_all(outs[1], outs[0], outs[3], outs[2])


def finish(own_rows, swapped, own_new, other_new):
    chips, block = swapped.shape[:2]
    return pl.pallas_call(
        finish_kernel,
        in_specs=[VMEM_SPEC] * 4,
        out_specs=[HBM_SPEC] * 4,
        out_shape=[
            jax.ShapeDtypeStruct(own_new.shape, jnp.float32),
            jax.ShapeDtypeStruct(own_new.shape, jnp.float32),
            jax.ShapeDtypeStruct(own_rows.shape, jnp.bfloat16),
            jax.ShapeDtypeStruct(own_rows.shape, jnp.bfloat16),
        ],
        scratch_shapes=[
            pltpu.VMEM((chips * block, LANES), jnp.float32),
            pltpu.VMEM(own_rows.shape, jnp.bfloat16),
            pltpu.SemaphoreType.DMA((11,)),
        ],
        compiler_params=SCOPED,
        name="finish",
    )(vmem(own_rows), vmem(swapped), vmem(own_new), vmem(other_new))


def body(client_deltas, variate_deltas, params, variate, taking_part, counts):
    first = my_core() == 0
    client_count = 2 * 128

    send = weigh(True, taking_part, counts, client_deltas, variate_deltas)
    came = core_swap(send)
    keep = weigh(False, taking_part, counts, client_deltas, variate_deltas)
    base = core_swap(jnp.where(first, variate, params))

    *quarters, own_quarter = join(keep, came)
    arrived = [lax.ppermute(vmem(q), AXIS, ring_pairs(k)) for q, k in zip(quarters, (1, 3, 2))]
    plane = fold([*arrived, own_quarter])
    blocks = lax.all_to_all(vmem(plane), AXIS, 0, 0, axis_index_groups=plane_groups(), tiled=True)
    own_new, sent_new, spread = update(blocks, params, variate, base, client_count)

    other_new = core_swap(sent_new)
    gathered = lax.all_to_all(spread, AXIS, 0, 0, axis_index_groups=chip_groups(), tiled=True)
    swapped = core_swap(gathered)
    own_rows = lay(gathered)
    return tuple(finish(own_rows, swapped, own_new, other_new))


def solution(mesh):
    flat = Mesh(mesh.devices.reshape(-1), (AXIS,))
    split = P(AXIS)
    in_specs = (split, split, split, split, split, split)
    out_specs = (split, split, P(), P())
    return jax.shard_map(body, mesh=flat, in_specs=in_specs, out_specs=out_specs, check_vma=False)
```

```python
import functools

import jax
import jax.numpy as jnp
from jax import lax
from jax.experimental import pallas as pl
from jax.experimental.pallas import tpu as pltpu
from jax.sharding import Mesh
from jax.sharding import PartitionSpec as P

AXIS = "d"
LANES = 128
CHIPS = 64


def device(i, core, s):
    return (i * 2 + core) * 8 + s


def place(d):
    return d // 16, d // 8 % 2, d % 8


def swap_pairs():
    pairs = []
    for d in range(128):
        i, core, s = place(d)
        pairs.append((d, device(i, 1 - core, s)))
    return pairs


def ring_pairs(step):
    pairs = []
    for d in range(128):
        i, core, s = place(d)
        if core == 0:
            pairs.append((d, device((i + 2 * step) % 8, core, s)))
        else:
            pairs.append((d, device(i, core, (s + 2 * step) % 8)))
    return pairs


def at(x, y, z, core):
    return device(2 * x + y // 2, core, 2 * z + y % 2)


FOUR = range(4)


def plane_groups():
    groups = [[at(x, y, z, 0) for y in FOUR for z in FOUR] for x in FOUR]
    return groups + [[at(x, y, z, 1) for y in FOUR for x in FOUR] for z in FOUR]


def chip_groups():
    first = [at(x, y, z, 0) for x in FOUR for y in FOUR for z in FOUR]
    return [first, [at(x, y, z, 1) for z in FOUR for y in FOUR for x in FOUR]]


def core_swap(x):
    return lax.ppermute(x, AXIS, swap_pairs())


def vmem(x):
    return pltpu.with_memory_space_constraint(x, pltpu.VMEM)


def hbm(x):
    return pltpu.with_memory_space_constraint(x, pltpu.HBM)


VMEM_SPEC = pl.BlockSpec(memory_space=pltpu.VMEM)
HBM_SPEC = pl.BlockSpec(memory_space=pltpu.HBM)
SCOPED = pltpu.CompilerParams(vmem_limit_bytes=8 * 2**20)


def my_core():
    return lax.axis_index(AXIS) // 8 % 2


def my_ring():
    d = lax.axis_index(AXIS)
    return jnp.where(d // 8 % 2 == 0, d // 32, d % 8 // 2)


STEPS = (1, 3, 2)


def tile_rows(columns):
    return -(-columns // LANES // 8) * 8


def weigh_kernel(
    other, taking_hbm, counts_hbm, deltas, changes, params, variate, out, *scratch
):
    held, taking, counts, row, arrived, small = scratch
    core = my_core()
    owner = 1 - core if other else core
    chunks, pieces = held.shape[0], held.shape[3] // LANES
    block = 2 * pieces
    group = 8 * block + 8

    def fetch(source):
        for i in range(chunks):
            pltpu.make_async_copy(
                source.at[:, pl.ds(16 * i, 16), :], held.at[i], arrived.at[i]
            ).start()

    def fill(a0, a1, tail, by_chunk, by_row):
        for g in range(8):
            out[pl.ds(g * group + 8 * block, 8), :] = jnp.full((8, LANES), tail)

        def one(i, carry):
            pltpu.make_async_copy(
                deltas.at[:, pl.ds(0, 16), :], held.at[i], arrived.at[i]
            ).wait()
            for half in range(2):
                rows = pl.ds(half * 8, 8)
                for j in range(pieces):
                    lanes = pl.ds(j * LANES, LANES)
                    value = held[i, 0, rows, lanes].astype(jnp.float32) * a0
                    value = value + held[i, 1, rows, lanes].astype(jnp.float32) * a1
                    start = i * by_chunk + half * pieces + j
                    out[pl.ds(start, 8, stride=by_row), :] = value
            return carry

        lax.fori_loop(0, chunks, one, 0)

    scalars = [
        pltpu.make_async_copy(taking_hbm, taking, small.at[0]),
        pltpu.make_async_copy(counts_hbm, counts, small.at[1]),
    ]
    for copy in scalars:
        copy.start()

    @pl.when(owner == 0)
    def _():
        fetch(deltas)
        pltpu.make_async_copy(params, row, small.at[2]).start()

    @pl.when(owner == 1)
    def _():
        fetch(changes)
        pltpu.make_async_copy(variate, row, small.at[2]).start()

    for copy in scalars:
        copy.wait()
    t0, t1 = taking[0], taking[1]
    w0, w1 = t0 * counts[0], t1 * counts[1]

    @pl.when(owner == 0)
    def _():
        total = (w0 + w1).astype(jnp.float32)
        fill(w0.astype(jnp.float32), w1.astype(jnp.float32), total, group, block)

    @pl.when(owner == 1)
    def _():
        fill(t0.astype(jnp.float32), t1.astype(jnp.float32), jnp.float32(0), block, group)

    pltpu.make_async_copy(params, row, small.at[2]).wait()
    for j in range(pieces):
        out[pl.ds(8 * group + j, 1), :] = row[:, pl.ds(j * LANES, LANES)]


def weigh(other, taking, counts, deltas, changes, params, variate):
    rows, columns = deltas.shape[1:]
    out_rows = 8 * (8 * 2 * columns // LANES + 8) + tile_rows(columns)
    return pl.pallas_call(
        functools.partial(weigh_kernel, other),
        in_specs=[HBM_SPEC] * 6,
        out_specs=VMEM_SPEC,
        out_shape=pltpu.VMEM((out_rows, LANES), jnp.float32),
        scratch_shapes=[
            pltpu.VMEM((rows // 16, 2, 16, columns), deltas.dtype),
            pltpu.SMEM(taking.shape, jnp.int32),
            pltpu.SMEM(counts.shape, jnp.int32),
            pltpu.VMEM(params.shape, jnp.float32),
            pltpu.SemaphoreType.DMA((rows // 16,)),
            pltpu.SemaphoreType.DMA((3,)),
        ],
        compiler_params=SCOPED,
        name="weigh_other" if other else "weigh_own",
    )(*[hbm(a) for a in (taking, counts, deltas, changes, params, variate)])


def join_kernel(keep, came, *outs):
    *parts, old = outs
    rows = parts[0].shape[0]
    mine = my_ring()
    for step, out in zip((*STEPS, 0), parts):
        at = pl.ds(pl.multiple_of((mine + step) % 4 * rows, 8), rows)
        out[...] = keep[at, :] + came[at, :]
    last = pl.ds(4 * rows, old.shape[1])
    old[0] = keep[last, :]
    old[1] = came[last, :]


def join(keep, came, columns):
    row = tile_rows(columns)
    part = pltpu.VMEM(((keep.shape[0] - row) // 4, LANES), jnp.float32)
    return pl.pallas_call(
        join_kernel,
        in_specs=[VMEM_SPEC, VMEM_SPEC],
        out_specs=[VMEM_SPEC] * 5,
        out_shape=[part] * 4 + [pltpu.VMEM((2, row, LANES), jnp.float32)],
        compiler_params=SCOPED,
        name="join",
    )(vmem(keep), vmem(came))


def fold_kernel(first, second, third, own, out):
    group = own.shape[0] // 2
    block = (group - 8) // 8
    swapped = my_core() == 1

    def total(start, size):
        here = pl.ds(start, size)
        return own[here, :] + first[here, :] + second[here, :] + third[here, :]

    tail = total(8 * block, 8)
    for g in range(2):
        for b in range(8):
            y = jnp.where(swapped, b % 2 * 2 + g, g * 2 + b % 2)
            start = pl.multiple_of((y * 4 + b // 2) * (block + 8), 8)
            out[pl.ds(start, block), :] = total(g * group + b * block, block)
            out[pl.ds(start + block, 8), :] = tail


def fold(parts):
    block = (parts[0].shape[0] // 2 - 8) // 8
    return pl.pallas_call(
        fold_kernel,
        in_specs=[VMEM_SPEC] * 4,
        out_specs=VMEM_SPEC,
        out_shape=pltpu.VMEM((16 * (block + 8), LANES), jnp.float32),
        compiler_params=SCOPED,
        name="fold",
    )(*[vmem(p) for p in parts]).reshape(16, block + 8, LANES)


def update_kernel(client_count, blocks, old, own, other, spread, total, fresh):
    core = my_core()
    count, used = blocks.shape[0], blocks.shape[1] - 8
    pieces = used // 2
    sums = blocks[0]
    for k in range(1, count):
        sums = sums + blocks[k]
    divisor = jnp.where(core == 0, sums[used : used + 1], jnp.float32(client_count))
    total[...] = sums[:used] / divisor
    for side, out in ((0, own), (1, other)):
        start = jnp.where(core == side, 0, pieces)
        for j in range(pieces):
            value = old[side, pl.ds(j, 1), :] + total[pl.ds(start + j, 1), :]
            out[:, pl.ds(j * LANES, LANES)] = value
            fresh[pl.ds(start + j, 1), :] = value
    rounded = fresh[...].astype(jnp.bfloat16)
    for k in range(CHIPS):
        spread[k] = rounded


def update(blocks, old, columns, client_count):
    used = blocks.shape[1] - 8
    row = pltpu.VMEM((1, columns), jnp.float32)
    return pl.pallas_call(
        functools.partial(update_kernel, client_count),
        in_specs=[VMEM_SPEC] * 2,
        out_specs=[VMEM_SPEC] * 3,
        out_shape=[row, row, pltpu.VMEM((CHIPS, used, LANES), jnp.bfloat16)],
        scratch_shapes=[pltpu.VMEM((used, LANES), jnp.float32)] * 2,
        compiler_params=SCOPED,
        name="update",
    )(vmem(blocks), vmem(old))


def lay_out(owner, source, wide, put, done=lambda i: None):
    block = source.shape[1]
    pieces = block // 2
    for far in FOUR:
        for near in FOUR:
            corner = jnp.where(owner == 0, far * 16 + near * 2, near * 16 + far * 2)
            for y in FOUR:
                start = pl.multiple_of((corner + y // 2 * 8 + y % 2) * block, 8)
                value = source[far * 16 + y * 4 + near]
                wide[pl.ds(start, block), :] = value.astype(jnp.float32)

    def one(i, carry):
        for j in range(pieces):
            rows = [wide[pl.ds(i * 8 * block + c * pieces + j, 8, stride=block), :] for c in (0, 1)]
            put(i, j, jnp.concatenate(rows).astype(jnp.bfloat16))
        done(i)
        return carry

    lax.fori_loop(0, 8, one, 0)


def lay_kernel(source, out, wide):
    def put(i, j, value):
        at = pl.ds(pl.multiple_of(i * 16, 16), 16)
        out[at, pl.ds(j * LANES, LANES)] = value

    lay_out(my_core(), source, wide, put)


def lay(gathered):
    chips, block = gathered.shape[:2]
    return pl.pallas_call(
        lay_kernel,
        in_specs=[VMEM_SPEC],
        out_specs=VMEM_SPEC,
        out_shape=pltpu.VMEM((2 * chips, block // 2 * LANES), jnp.bfloat16),
        scratch_shapes=[pltpu.VMEM((chips * block, LANES), jnp.float32)],
        compiler_params=SCOPED,
        name="lay",
    )(vmem(gathered))


def finish_kernel(own_rows, swapped, own_new, other_new, *refs):
    outs, wide, laid, sems = refs[:4], refs[4], refs[5], refs[6]
    core = my_core()

    def place_all(mine, theirs, mine_rows, their_rows):
        copies = [
            pltpu.make_async_copy(own_new, mine, sems.at[0]),
            pltpu.make_async_copy(other_new, theirs, sems.at[1]),
            pltpu.make_async_copy(own_rows, mine_rows, sems.at[2]),
        ]
        for copy in copies:
            copy.start()

        def put(i, j, value):
            at = pl.ds(pl.multiple_of(i * 16, 16), 16)
            laid[at, pl.ds(j * LANES, LANES)] = value

        def write(i):
            at = pl.ds(pl.multiple_of(i * 16, 16), 16)
            return pltpu.make_async_copy(laid.at[at, :], their_rows.at[at, :], sems.at[3 + i])

        lay_out(1 - core, swapped, wide, put, lambda i: write(i).start())
        for copy in copies:
            copy.wait()
        for i in range(8):
            write(i).wait()

    @pl.when(core == 0)
    def _():
        place_all(outs[0], outs[1], outs[2], outs[3])

    @pl.when(core == 1)
    def _():
        place_all(outs[1], outs[0], outs[3], outs[2])


def finish(own_rows, swapped, own_new, other_new):
    chips, block = swapped.shape[:2]
    return pl.pallas_call(
        finish_kernel,
        in_specs=[VMEM_SPEC] * 4,
        out_specs=[HBM_SPEC] * 4,
        out_shape=[
            jax.ShapeDtypeStruct(own_new.shape, jnp.float32),
            jax.ShapeDtypeStruct(own_new.shape, jnp.float32),
            jax.ShapeDtypeStruct(own_rows.shape, jnp.bfloat16),
            jax.ShapeDtypeStruct(own_rows.shape, jnp.bfloat16),
        ],
        scratch_shapes=[
            pltpu.VMEM((chips * block, LANES), jnp.float32),
            pltpu.VMEM(own_rows.shape, jnp.bfloat16),
            pltpu.SemaphoreType.DMA((11,)),
        ],
        compiler_params=SCOPED,
        name="finish",
    )(vmem(own_rows), vmem(swapped), vmem(own_new), vmem(other_new))


def body(client_deltas, variate_deltas, params, variate, taking_part, counts):
    client_count = 2 * 128
    columns = params.shape[1]
    arguments = (taking_part, counts, client_deltas, variate_deltas, params, variate)

    came = core_swap(weigh(True, *arguments))
    keep = weigh(False, *arguments)
    *sent, own, old = join(keep, came, columns)
    sent = [lax.ppermute(vmem(p), AXIS, ring_pairs(k)) for p, k in zip(sent, STEPS)]
    plane = fold([*sent, own])
    blocks = lax.all_to_all(plane, AXIS, 0, 0, axis_index_groups=plane_groups(), tiled=True)
    own_new, sent_new, spread = update(blocks, old, columns, client_count)

    other_new = core_swap(sent_new)
    gathered = lax.all_to_all(spread, AXIS, 0, 0, axis_index_groups=chip_groups(), tiled=True)
    swapped = core_swap(gathered)
    own_rows = lay(gathered)
    return tuple(finish(own_rows, swapped, own_new, other_new))


def solution(mesh):
    flat = Mesh(mesh.devices.reshape(-1), (AXIS,))
    split = P(AXIS)
    in_specs = (split, split, split, split, split, split)
    out_specs = (split, split, P(), P())
    return jax.shard_map(body, mesh=flat, in_specs=in_specs, out_specs=out_specs, check_vma=False)
```
